512 devices in a mesh: branch: 64 (over x, z_lo, y), head: 8 (over z_hi, core).
Axes of the slice: x: 4, y: 8, z: 8 (z_hi: 4, z_lo: 2; z = z_hi * 2 + z_lo), core: 2. Of those that a mesh axis runs over, the one named last changes fastest.
Arguments:
- queries: bfloat16 [16384, 8192], P('branch', 'head'), may hold values from -8 to 8
- branch_keys: bfloat16 [16384, 1024], P('branch', 'head'), may hold values from -6 to 6
- branch_values: bfloat16 [16384, 1024], P('branch', 'head'), may hold values from -6 to 6
- prompt_keys: bfloat16 [3072, 1024], P(('branch', 'head')), may hold values from -6 to 6
- prompt_values: bfloat16 [3072, 1024], P(('branch', 'head')), may hold values from -6 to 6
- parent: int32 [64], replicated, may hold values from -1 to 63, as said below
- fork_tokens: int32 [64], replicated, may hold values from 0 to 256, as said below
- lengths: int32 [64], replicated, may hold values from 64 to 256
Outputs:
- attended: bfloat16 [16384, 8192], P('branch', 'head')
The draws below stay inside these ranges and needn't reach their ends.
Inputs may be any that keep to these rules, and one draw needn't show every extreme that they name: Exactly 8 branches have parent -1, and every other branch's parent is one of them. `fork_tokens`: 0 where parent is -1, else at most the parent's length.
All inputs are finite; a program needn't handle non-finite values.
Results may differ from the reference program's by a relative error of at most 0.0045.
Values may be sent and summed in bfloat16 or wider, within the bound.
No kernel may reach another device: no remote copies, remote signals or barrier semaphores. Data moves between devices by JAX's collectives and lax.ppermute only.
A program may use at most 64 MiB of HBM per device.

```python
import math
import jax
import jax.numpy as jnp
from jax import lax

HEADS = 64
KV_HEADS = 8
HEAD_DIM = 128
TOK = 256
NB = 64
PROMPT = 3072


def tree_draw(key):
    folded = jax.random.fold_in(key, 7)
    key_perm, key_len, key_limit, key_slot, key_fork = jax.random.split(folded, 5)
    order_table = jax.random.permutation(key_perm, NB).astype(jnp.int32)
    positions = jnp.arange(NB, dtype=jnp.int32)
    last_at = jnp.sum(jnp.where(order_table == NB - 1, positions, 0)).astype(jnp.int32)
    first_entry = order_table[0]
    order_table = order_table.at[last_at].set(first_entry).at[0].set(NB - 1).astype(jnp.int32)
    ranking = jnp.argsort(order_table, stable=True).astype(jnp.int32)
    root_count = NB // 8
    is_root = ranking < root_count
    lengths = jax.random.randint(key_len, (NB,), TOK // 4, TOK + 1).astype(jnp.int32)
    lengths = lengths.at[order_table[0]].set(TOK).at[order_table[1]].set(TOK // 4)
    slot_limit = jax.random.randint(key_limit, (NB,), 1, root_count + 1)
    slot_pick = jax.random.randint(key_slot, (NB,), 0, slot_limit)
    slot_pick = jnp.where(ranking == root_count, 0, slot_pick)
    parent = jnp.where(is_root, -1, order_table[slot_pick]).astype(jnp.int32)
    parent_safe = jnp.maximum(parent, 0)
    fork_tokens = jax.random.randint(key_fork, (NB,), 1, lengths[parent_safe] + 1)
    fork_tokens = jnp.where(ranking == root_count, TOK, fork_tokens)
    fork_tokens = jnp.where(is_root, 0, fork_tokens).astype(jnp.int32)
    return (parent, fork_tokens, lengths, ranking)


def draw_parent(key, part):
    return tree_draw(key)[0]


def draw_fork_tokens(key, part):
    return tree_draw(key)[1]


def draw_lengths(key, part):
    return tree_draw(key)[2]


def query_damping(key):
    ranking = tree_draw(key)[3]
    root_count = NB // 8
    damped = (ranking % 4 == 0) | (ranking == root_count)
    row_branch = jnp.arange(NB * TOK, dtype=jnp.int32) // TOK
    return jnp.where(damped[row_branch], 0.25, 1.0).astype(jnp.float32)


def draw_queries(key, part):
    folded = jax.random.fold_in(key, 13)
    shape_full = (NB * TOK, HEADS * HEAD_DIM)
    damping = query_damping(key)
    drawn = jnp.clip(2.5 * jax.random.normal(folded, shape_full, jnp.float32), -8.0, 8.0)
    drawn = drawn * damping[:, None]
    return drawn.astype(jnp.bfloat16)


def draw_prompt_keys(key, part):
    folded = jax.random.fold_in(key, 17)
    shape_full = (PROMPT, KV_HEADS * HEAD_DIM)
    drawn = jnp.clip(jax.random.normal(folded, shape_full, jnp.float32), -6.0, 6.0)
    return drawn.astype(jnp.bfloat16)


def level_of(stream_key, shape, cuts, low, largest):
    def one(dim, blocks):
        heights = jax.random.uniform(jax.random.fold_in(jax.random.fold_in(stream_key, 6), dim), (blocks,), jnp.float32, low / len(cuts), largest / len(cuts))
        return jnp.repeat(jnp.exp(heights), shape[dim] // blocks).reshape((-1,) + (1,) * (len(shape) - dim - 1))

    factor_of = one(*cuts[0])
    for cut in cuts[1:]:
        factor_of = factor_of * one(*cut)
    return factor_of


def centred(own_key, extent, spread, bound, cuts=(), kind=jnp.bfloat16):
    level = level_of(own_key, extent, cuts, -0.22, 0.18) if cuts else 1.0
    entries = jax.random.normal(own_key, extent, jnp.float32) * spread * level
    return jnp.minimum(jnp.maximum(entries, -bound), bound).astype(kind)


def setup_inputs(seed: int = 0) -> dict:
    key_of = jax.random.split(jax.random.key(seed), 9)
    queries = draw_queries(jax.random.fold_in(key_of[8], 71), 0)
    branch_keys = centred(key_of[1], (NB * TOK, KV_HEADS * HEAD_DIM), 1.0, 6.0, ((0, 64), (1, 8)))
    branch_values = centred(key_of[2], (NB * TOK, KV_HEADS * HEAD_DIM), 1.0, 6.0, ((0, 64), (1, 8)))
    prompt_keys = draw_prompt_keys(jax.random.fold_in(key_of[8], 71), 0)
    prompt_values = centred(key_of[4], (PROMPT, KV_HEADS * HEAD_DIM), 1.0, 6.0, ((0, 512),))
    parent = draw_parent(jax.random.fold_in(key_of[8], 71), 0)
    fork_tokens = draw_fork_tokens(jax.random.fold_in(key_of[8], 71), 0)
    lengths = draw_lengths(jax.random.fold_in(key_of[8], 71), 0)
    return dict(queries=queries, branch_keys=branch_keys, branch_values=branch_values, prompt_keys=prompt_keys, prompt_values=prompt_values, parent=parent, fork_tokens=fork_tokens, lengths=lengths)


def reference(queries, branch_keys, branch_values, prompt_keys, prompt_values, parent, fork_tokens, lengths):
    branches = parent.shape[0]
    tok_rows = queries.shape[0] // branches
    groups = KV_HEADS
    per_group = HEADS // KV_HEADS
    score_scale = 1.0 / math.sqrt(HEAD_DIM)
    prompt_len = prompt_keys.shape[0]
    prompt_key_f = prompt_keys.astype(jnp.float32).reshape(prompt_len, groups, HEAD_DIM)
    prompt_value_f = prompt_values.astype(jnp.float32).reshape(prompt_len, groups, HEAD_DIM)
    query_pos = jnp.arange(tok_rows, dtype=jnp.int32)

    def take_rows(source, first):
        return lax.dynamic_slice_in_dim(source, first, tok_rows, 0).astype(jnp.float32).reshape(tok_rows, groups, HEAD_DIM)

    def per_branch(branch):
        row_start = (branch * tok_rows).astype(jnp.int32)
        parent_id = parent[branch]
        parent_start = (jnp.maximum(parent_id, 0) * tok_rows).astype(jnp.int32)
        query_f = lax.dynamic_slice_in_dim(queries, row_start, tok_rows, 0).astype(jnp.float32)
        query_f = query_f.reshape(tok_rows, groups, per_group, HEAD_DIM)
        key_all = jnp.concatenate([prompt_key_f, take_rows(branch_keys, parent_start), take_rows(branch_keys, row_start)], 0)
        value_all = jnp.concatenate([prompt_value_f, take_rows(branch_values, parent_start), take_rows(branch_values, row_start)], 0)
        from_parent = (parent_id >= 0) & (query_pos < fork_tokens[branch])
        visible = jnp.concatenate([jnp.ones((tok_rows, prompt_len), dtype=bool), jnp.broadcast_to(from_parent[None, :], (tok_rows, tok_rows)), query_pos[None, :] <= query_pos[:, None]], 1)
        scores = jnp.einsum('tgqd,ngd->tgqn', query_f, key_all) * score_scale
        scores = jnp.where(visible[:, None, None, :], scores, -jnp.inf)
        row_max = lax.optimization_barrier(jnp.max(scores, axis=-1, keepdims=True))
        weights = jnp.exp(scores - row_max)
        denominator = lax.optimization_barrier(jnp.sum(weights, axis=-1))
        weights_low = lax.optimization_barrier(weights.astype(jnp.bfloat16)).astype(jnp.float32)
        numerator = jnp.einsum('tgqn,ngd->tgqd', weights_low, value_all)
        output = numerator / denominator[..., None]
        live = query_pos < lengths[branch]
        output = jnp.where(live[:, None, None, None], output, 0.0)
        return output.reshape(tok_rows, HEADS * HEAD_DIM).astype(jnp.bfloat16)
    results = lax.map(per_branch, jnp.arange(branches, dtype=jnp.int32))
    return results.reshape(branches * tok_rows, HEADS * HEAD_DIM)
```

```python
import math

import jax
import jax.numpy as jnp
from jax import lax
from jax.experimental import pallas as pl
from jax.experimental.pallas import tpu as pltpu
from jax.sharding import Mesh, PartitionSpec as P

HEADS = 64
KV_HEADS = 8
HEAD_DIM = 128
PER_GROUP = HEADS // KV_HEADS
SCALE2 = math.log2(math.e) / math.sqrt(HEAD_DIM)
NEG = -1e30
BRANCH = ("x", "zl", "y")
PLANE = ("x", "zl")
HEAD = ("zh", "c")
CONTRACT_LAST = (((1,), (1,)), ((), ()))
CONTRACT_MID = (((1,), (0,)), ((), ()))


def scores_of(q, k):
    return lax.dot_general(q, k, CONTRACT_LAST, preferred_element_type=jnp.float32)


def attend_kernel(meta, q_ref, prompt_ref, own_k, own_v, parent_ref, o_ref):
    tok = q_ref.shape[0]
    q = q_ref[...]
    groups, rows = prompt_ref.shape[0], prompt_ref.shape[1] // 2
    col = lax.broadcasted_iota(jnp.int32, (tok, tok), 1)
    row = lax.broadcasted_iota(jnp.int32, (tok, tok), 0)
    parts = []
    for i in range(groups):
        parts.append((scores_of(q, prompt_ref[i, :rows]), prompt_ref[i, rows:]))
    own = jnp.where(col <= row, scores_of(q, own_k[...]), NEG)
    parts.append((own, own_v[...]))
    up = jnp.where(col < meta[0], scores_of(q, parent_ref[:tok]), NEG)
    parts.append((up, parent_ref[tok:]))
    top = None
    for s, _ in parts:
        peak = jnp.max(s, axis=1, keepdims=True)
        top = peak if top is None else jnp.maximum(top, peak)
    total = jnp.zeros((tok, 1), jnp.float32)
    acc = jnp.zeros((tok, HEAD_DIM), jnp.float32)
    for s, v in parts:
        w = jnp.exp2((s - top) * SCALE2)
        total += jnp.sum(w, axis=1, keepdims=True)
        acc += lax.dot_general(
            w.astype(jnp.bfloat16), v, CONTRACT_MID, preferred_element_type=jnp.float32
        )
    live = lax.broadcasted_iota(jnp.int32, (tok, HEAD_DIM), 0) < meta[1]
    o_ref[...] = jnp.where(live, acc / total, 0.0).astype(o_ref.dtype)


def attend(meta, queries, prompt, own_k, own_v, parent_kv):
    tok, width = queries.shape
    whole = lambda a: pl.BlockSpec(a.shape, lambda h, *_: (0,) * a.ndim)
    head = pl.BlockSpec((tok, HEAD_DIM), lambda h, *_: (0, h))
    keys = prompt.shape[0] * prompt.shape[1] // 2 + 2 * tok
    return pl.pallas_call(
        attend_kernel,
        out_shape=jax.ShapeDtypeStruct((tok, width), jnp.bfloat16),
        grid_spec=pltpu.PrefetchScalarGridSpec(
            num_scalar_prefetch=1,
            grid=(width // HEAD_DIM,),
            in_specs=[head, whole(prompt), whole(own_k), whole(own_v), whole(parent_kv)],
            out_specs=head,
        ),
        compiler_params=pltpu.CompilerParams(vmem_limit_bytes=48 << 20),
        cost_estimate=pl.CostEstimate(
            flops=4 * tok * width * keys,
            transcendentals=tok * (width // HEAD_DIM) * keys,
            bytes_accessed=4 * tok * width + 4 * keys * HEAD_DIM,
        ),
    )(meta, queries, prompt, own_k, own_v, parent_kv)


def body(queries, branch_keys, branch_values, prompt_keys, prompt_values, parent, fork, lengths):
    tok = queries.shape[0]
    rows = prompt_keys.shape[0]
    ny = lax.axis_size("y")
    nh = lax.axis_size(HEAD)
    nb = lax.axis_size(BRANCH)
    me = lax.axis_index(BRANCH)

    own = jnp.concatenate([branch_keys, branch_values], 0).reshape(nb, 2 * tok // nb, HEAD_DIM)
    pieces = lax.all_to_all(own, BRANCH, split_axis=0, concat_axis=0, tiled=True)
    chosen = pieces.at[jnp.maximum(parent, 0)].get(mode="promise_in_bounds")
    parent_kv = lax.all_to_all(chosen, BRANCH, split_axis=0, concat_axis=0, tiled=True)
    parent_kv = parent_kv.reshape(2 * tok, HEAD_DIM)

    split = lambda a: a.reshape(rows, nh, HEAD_DIM).transpose(1, 0, 2)
    mine = jnp.concatenate([split(prompt_keys), split(prompt_values)], 1)
    spread = jnp.broadcast_to(mine[None], (ny,) + mine.shape).reshape(ny * nh, 2 * rows, HEAD_DIM)
    line = lax.all_to_all(spread, ("y",) + HEAD, split_axis=0, concat_axis=0, tiled=True)
    part = lambda a: a.reshape(ny * nh * rows, HEAD_DIM)
    line = jnp.concatenate([part(line[:, :rows]), part(line[:, rows:])], 0)
    plane = lax.axis_size(PLANE)
    spread = jnp.broadcast_to(line[None], (plane,) + line.shape)
    prompt = lax.all_to_all(spread, PLANE, split_axis=0, concat_axis=0, tiled=True)

    meta = jnp.stack([fork[me], lengths[me]])
    return attend(meta, queries, prompt, branch_keys, branch_values, parent_kv)


def solution(mesh):
    fine = Mesh(mesh.devices.reshape(4, 2, 8, 4, 2), BRANCH + HEAD)
    placed = (
        P(BRANCH, HEAD),
        P(BRANCH, HEAD),
        P(BRANCH, HEAD),
        P(BRANCH + HEAD, None),
        P(BRANCH + HEAD, None),
        P(),
        P(),
        P(),
    )
    return jax.shard_map(
        body, mesh=fine, in_specs=placed, out_specs=P(BRANCH, HEAD), check_vma=False
    )
```

```python
import functools
import math

import jax
import jax.numpy as jnp
from jax import lax
from jax.experimental import pallas as pl
from jax.experimental.pallas import tpu as pltpu
from jax.sharding import Mesh, PartitionSpec as P

HEAD_DIM = 128
SCALE2 = math.log2(math.e) / math.sqrt(HEAD_DIM)
NEG = -1e30
CHUNK = 512
BRANCH = ("x", "zl", "y")
PLANE = ("x", "zl")
HEAD = ("zh", "c")
CONTRACT_LAST = (((1,), (1,)), ((), ()))
CONTRACT_MID = (((1,), (0,)), ((), ()))


def absorb(q, parts, state):
    for k, v, mask in parts:
        s = lax.dot_general(q, k, CONTRACT_LAST, preferred_element_type=jnp.float32)
        if mask is not None:
            s = jnp.where(mask, s, NEG)
        top = jnp.max(s, axis=1, keepdims=True)
        if state is not None:
            top = jnp.maximum(state[0], top)
        w = jnp.exp2((s - top) * SCALE2).astype(jnp.bfloat16)
        both = lax.dot_general(
            w,
            jnp.concatenate([v, jnp.ones_like(v)], 1),
            CONTRACT_MID,
            preferred_element_type=jnp.float32,
        )
        acc, total = both[:, :HEAD_DIM], both[:, HEAD_DIM:]
        if state is not None:
            fade = jnp.exp2((state[0] - top) * SCALE2)
            total += state[1] * fade
            acc += state[2] * fade
        state = (top, total, acc)
    return state


def stacked(ref):
    return jnp.concatenate(
        [ref[:, i : i + HEAD_DIM] for i in range(0, ref.shape[1], HEAD_DIM)], 0
    )


def store_state(state, acc_ref, stat_ref, heads):
    top, total, acc = state
    tok = acc_ref.shape[0]
    here = acc_ref.shape[1] // HEAD_DIM
    step = pl.program_id(0)
    lane = lax.broadcasted_iota(jnp.int32, (tok, HEAD_DIM), 1)
    stat = stat_ref[...]
    for i in range(here):
        at = slice(i * tok, (i + 1) * tok)
        acc_ref[:, i * HEAD_DIM : (i + 1) * HEAD_DIM] = acc[at]
        stat = jnp.where(lane == step * here + i, top[at], stat)
        stat = jnp.where(lane == heads + step * here + i, total[at], stat)
    stat_ref[...] = stat


def load_state(acc_ref, stat_ref, heads):
    here = acc_ref.shape[1] // HEAD_DIM
    step = pl.program_id(0)
    stat = stat_ref[...]
    lane = lax.broadcasted_iota(jnp.int32, stat.shape, 1)
    pick = lambda j: jnp.sum(jnp.where(lane == j, stat, 0.0), axis=1, keepdims=True)
    top = jnp.concatenate([pick(step * here + i) for i in range(here)], 0)
    total = jnp.concatenate([pick(heads + step * here + i) for i in range(here)], 0)
    return top, total, stacked(acc_ref)


def first_kernel(q_ref, own_k, own_v, line_ref, acc_ref, stat_ref, *, heads):
    tok = q_ref.shape[0]
    half = line_ref.shape[0] // 2
    q = stacked(q_ref)
    shape = (q.shape[0], tok)
    row = lax.rem(lax.broadcasted_iota(jnp.int32, shape, 0), tok)
    causal = lax.broadcasted_iota(jnp.int32, shape, 1) <= row
    parts = [
        (line_ref[:half], line_ref[half:], None),
        (own_k[...], own_v[...], causal),
    ]
    store_state(absorb(q, parts, None), acc_ref, stat_ref, heads)


def prompt_kernel(
    me, q_ref, whole_ref, acc_in, stat_in, acc_ref, stat_ref, keys, values, *, heads, half
):
    plane = whole_ref.shape[0]

    @pl.when(pl.program_id(0) == 0)
    def _():
        for i in range(1, plane):
            g = lax.rem(me[0] + i, plane)
            at = slice((i - 1) * half, i * half)
            keys[at] = whole_ref[g, :half]
            values[at] = whole_ref[g, half : 2 * half]

    parts = []
    for i in range(0, keys.shape[0], CHUNK):
        at = slice(i, min(i + CHUNK, keys.shape[0]))
        parts.append((keys[at], values[at], None))
    state = absorb(stacked(q_ref), parts, load_state(acc_in, stat_in, heads))
    store_state(state, acc_ref, stat_ref, heads)


def last_kernel(me, fork, lengths, q_ref, above_ref, acc_in, stat_in, o_ref, *, heads):
    tok = q_ref.shape[0]
    q = stacked(q_ref)
    seen = lax.broadcasted_iota(jnp.int32, (q.shape[0], tok), 1) < fork[me[1]]
    parts = [(above_ref[:tok], above_ref[tok:], seen)]
    _, total, acc = absorb(q, parts, load_state(acc_in, stat_in, heads))
    kept = lax.broadcasted_iota(jnp.int32, (tok, HEAD_DIM), 0) < lengths[me[1]]
    out = acc / total
    for i in range(q_ref.shape[1] // HEAD_DIM):
        at = slice(i * HEAD_DIM, (i + 1) * HEAD_DIM)
        o_ref[:, at] = jnp.where(kept, out[i * tok : (i + 1) * tok], 0.0).astype(o_ref.dtype)


def attention(kernel, name, q, tables, shared, state, outs, keys, per_step, scratch=()):
    tok, width = q.shape
    step = per_step * HEAD_DIM
    fixed = lambda a: pl.BlockSpec(a.shape, lambda h, *_: (0,) * a.ndim)
    moving = pl.BlockSpec((tok, step), lambda h, *_: (0, h))
    spec = lambda a: moving if a.shape[1] == width else fixed(a)
    return pl.pallas_call(
        kernel,
        name=name,
        out_shape=outs,
        grid_spec=pltpu.PrefetchScalarGridSpec(
            num_scalar_prefetch=len(tables),
            grid=(width // step,),
            in_specs=[moving] + [fixed(a) for a in shared] + [spec(a) for a in state],
            out_specs=jax.tree.map(spec, outs),
            scratch_shapes=scratch,
        ),
        compiler_params=pltpu.CompilerParams(vmem_limit_bytes=40 << 20),
        cost_estimate=pl.CostEstimate(
            flops=4 * tok * width * keys,
            transcendentals=tok * (width // HEAD_DIM) * keys,
            bytes_accessed=4 * tok * width + 4 * keys * HEAD_DIM,
        ),
    )(*tables, q, *shared, *state)


def choose_kernel(parent, whole_ref, o_ref, *, start):
    count, unit = o_ref.shape[0], o_ref.shape[1]
    each = count // whole_ref.shape[0]
    for b in range(count):
        p = jnp.maximum(parent[b], 0)
        at = pl.multiple_of(start + lax.rem(p, each) * unit, unit)
        o_ref[b] = whole_ref[p // each, pl.ds(at, unit)]


def exchange(a, axes):
    return lax.all_to_all(a, axes, split_axis=0, concat_axis=0, tiled=True)


def body(queries, branch_keys, branch_values, prompt_keys, prompt_values, parent, fork, lengths):
    tok, width = queries.shape
    heads = width // HEAD_DIM
    rows = prompt_keys.shape[0]
    ny, nh, nb = lax.axis_size("y"), lax.axis_size(HEAD), lax.axis_size(BRANCH)
    plane = lax.axis_size(PLANE)
    unit = 2 * tok // nb
    where = jnp.stack([lax.axis_index(PLANE), lax.axis_index(BRANCH)])

    split = lambda a: a.reshape(rows, nh, HEAD_DIM).transpose(1, 0, 2)
    mine = exchange(jnp.concatenate([split(prompt_keys), split(prompt_values)], 1), HEAD)
    half = nh * rows
    part = lambda a: a.reshape(half, HEAD_DIM)
    mine = jnp.concatenate([part(mine[:, :rows]), part(mine[:, rows:])], 0)
    own = jnp.concatenate([branch_keys, branch_values], 0)
    own = own.reshape(plane, ny, unit, HEAD_DIM).transpose(1, 0, 2, 3)
    own = own.reshape(ny, plane * unit, HEAD_DIM)
    spread = jnp.broadcast_to(mine[None], (ny,) + mine.shape)
    line = exchange(jnp.concatenate([spread, own], 1), "y")

    part = lambda a: a.reshape(ny * half, HEAD_DIM)
    prompt = jnp.concatenate([part(line[:, :half]), part(line[:, half : 2 * half])], 0)
    pieces = line[:, 2 * half :].reshape(ny, plane, unit, HEAD_DIM).transpose(1, 0, 2, 3)
    pieces = pieces.reshape(plane, ny * unit, HEAD_DIM)
    spread = jnp.broadcast_to(prompt[None], (plane,) + prompt.shape)
    whole = exchange(jnp.concatenate([spread, pieces], 1), PLANE)

    half = ny * half
    chosen = pl.pallas_call(
        functools.partial(choose_kernel, start=2 * half),
        name="choose",
        out_shape=jax.ShapeDtypeStruct((nb, unit, HEAD_DIM), jnp.bfloat16),
        in_specs=[
            pl.BlockSpec(memory_space=pltpu.SMEM),
            pl.BlockSpec(memory_space=pltpu.VMEM),
        ],
        out_specs=pl.BlockSpec(memory_space=pltpu.VMEM),
        compiler_params=pltpu.CompilerParams(vmem_limit_bytes=4 << 20),
    )(parent, whole)
    above = exchange(chosen, BRANCH).reshape(2 * tok, HEAD_DIM)

    state = (
        jax.ShapeDtypeStruct((tok, width), jnp.float32),
        jax.ShapeDtypeStruct((tok, HEAD_DIM), jnp.float32),
    )
    bound = lambda kernel, **more: functools.partial(kernel, heads=heads, **more)
    carried = attention(
        bound(first_kernel),
        "first",
        queries,
        (),
        (branch_keys, branch_values, prompt),
        (),
        state,
        tok + half,
        4,
    )
    rest = (plane - 1) * half
    carried = attention(
        bound(prompt_kernel, half=half),
        "rest",
        queries,
        (where,),
        (whole,),
        carried,
        state,
        rest,
        4,
        [pltpu.VMEM((rest, HEAD_DIM), jnp.bfloat16)] * 2,
    )
    out = jax.ShapeDtypeStruct((tok, width), jnp.bfloat16)
    return attention(
        bound(last_kernel),
        "last",
        queries,
        (where, fork, lengths),
        (above,),
        carried,
        out,
        tok,
        4,
    )


def solution(mesh):
    fine = Mesh(mesh.devices.reshape(4, 2, 8, 4, 2), BRANCH + HEAD)
    placed = (
        P(BRANCH, HEAD),
        P(BRANCH, HEAD),
        P(BRANCH, HEAD),
        P(BRANCH + HEAD, None),
        P(BRANCH + HEAD, None),
        P(),
        P(),
        P(),
    )
    return jax.shard_map(
        body, mesh=fine, in_specs=placed, out_specs=P(BRANCH, HEAD), check_vma=False
    )
```

```python
import functools
import math

import jax
import jax.numpy as jnp
from jax import lax
from jax.experimental import pallas as pl
from jax.experimental.pallas import tpu as pltpu
from jax.sharding import Mesh, PartitionSpec as P


HEAD_DIM = 128
SCALE2 = math.log2(math.e) / math.sqrt(HEAD_DIM)
NEG = -1e30
CHUNK = 512
BRANCH = ("x", "zl", "y")
HEAD = ("zh", "c")
CONTRACT_LAST = (((1,), (1,)), ((), ()))
CONTRACT_MID = (((1,), (0,)), ((), ()))


def absorb(q, parts, state):
    for k, v, mask in parts:
        s = lax.dot_general(q, k, CONTRACT_LAST, preferred_element_type=jnp.float32)
        if mask is not None:
            s = jnp.where(mask, s, NEG)
        top = jnp.max(s, axis=1, keepdims=True)
        if state is not None:
            top = jnp.maximum(state[0], top)
        w = jnp.exp2((s - top) * SCALE2).astype(jnp.bfloat16)
        both = lax.dot_general(
            w,
            jnp.concatenate([v, jnp.ones_like(v)], 1),
            CONTRACT_MID,
            preferred_element_type=jnp.float32,
        )
        acc, total = both[:, :HEAD_DIM], both[:, HEAD_DIM:]
        if state is not None:
            fade = jnp.exp2((state[0] - top) * SCALE2)
            total += state[1] * fade
            acc += state[2] * fade
        state = (top, total, acc)
    return state


def stacked(ref):
    return jnp.concatenate(
        [ref[:, i : i + HEAD_DIM] for i in range(0, ref.shape[1], HEAD_DIM)], 0
    )


def store_state(state, acc_ref, stat_ref, heads):
    top, total, acc = state
    tok = acc_ref.shape[0]
    here = acc_ref.shape[1] // HEAD_DIM
    step = pl.program_id(0)
    lane = lax.broadcasted_iota(jnp.int32, (tok, HEAD_DIM), 1)
    stat = stat_ref[...]
    for i in range(here):
        at = slice(i * tok, (i + 1) * tok)
        acc_ref[:, i * HEAD_DIM : (i + 1) * HEAD_DIM] = acc[at]
        stat = jnp.where(lane == step * here + i, top[at], stat)
        stat = jnp.where(lane == heads + step * here + i, total[at], stat)
    stat_ref[...] = stat


def load_state(acc_ref, stat_ref, heads):
    here = acc_ref.shape[1] // HEAD_DIM
    step = pl.program_id(0)
    stat = stat_ref[...]
    lane = lax.broadcasted_iota(jnp.int32, stat.shape, 1)
    pick = lambda j: jnp.sum(jnp.where(lane == j, stat, 0.0), axis=1, keepdims=True)
    top = jnp.concatenate([pick(step * here + i) for i in range(here)], 0)
    total = jnp.concatenate([pick(heads + step * here + i) for i in range(here)], 0)
    return top, total, stacked(acc_ref)


def prompt_kernel(q_ref, *refs, heads):
    blocks, (own_k, own_v, acc_ref, stat_ref, keys, values) = refs[:-6], refs[-6:]
    tok = q_ref.shape[0]

    @pl.when(pl.program_id(0) == 0)
    def _():
        start = 0
        for block in blocks:
            half = block.shape[1] // 2
            for i in range(block.shape[0]):
                keys[start : start + half] = block[i, :half]
                values[start : start + half] = block[i, half:]
                start += half

    q = stacked(q_ref)
    shape = (q.shape[0], tok)
    row = lax.rem(lax.broadcasted_iota(jnp.int32, shape, 0), tok)
    causal = lax.broadcasted_iota(jnp.int32, shape, 1) <= row
    parts = [
        (keys[i : i + CHUNK], values[i : i + CHUNK], None) for i in range(0, keys.shape[0], CHUNK)
    ]
    parts.append((own_k[...], own_v[...], causal))
    store_state(absorb(q, parts, None), acc_ref, stat_ref, heads)


def last_kernel(me, fork, lengths, q_ref, above_ref, acc_in, stat_in, o_ref, *, heads):
    tok = q_ref.shape[0]
    q = stacked(q_ref)
    seen = lax.broadcasted_iota(jnp.int32, (q.shape[0], tok), 1) < fork[me[0]]
    parts = [(above_ref[:tok], above_ref[tok:], seen)]
    _, total, acc = absorb(q, parts, load_state(acc_in, stat_in, heads))
    kept = lax.broadcasted_iota(jnp.int32, (tok, HEAD_DIM), 0) < lengths[me[0]]
    out = acc / total
    for i in range(q_ref.shape[1] // HEAD_DIM):
        at = slice(i * HEAD_DIM, (i + 1) * HEAD_DIM)
        o_ref[:, at] = jnp.where(kept, out[i * tok : (i + 1) * tok], 0.0).astype(o_ref.dtype)


def attention(kernel, q, tables, shared, state, outs, keys, per_step, scratch=()):
    tok, width = q.shape
    step = per_step * HEAD_DIM
    fixed = lambda a: pl.BlockSpec(a.shape, lambda h, *_: (0,) * a.ndim)
    moving = pl.BlockSpec((tok, step), lambda h, *_: (0, h))
    spec = lambda a: moving if a.shape[1] == width else fixed(a)
    return pl.pallas_call(
        kernel,
        out_shape=outs,
        grid_spec=pltpu.PrefetchScalarGridSpec(
            num_scalar_prefetch=len(tables),
            grid=(width // step,),
            in_specs=[moving] + [fixed(a) for a in shared] + [spec(a) for a in state],
            out_specs=jax.tree.map(spec, outs),
            scratch_shapes=scratch,
        ),
        compiler_params=pltpu.CompilerParams(vmem_limit_bytes=40 << 20),
        cost_estimate=pl.CostEstimate(
            flops=4 * tok * width * keys,
            transcendentals=tok * (width // HEAD_DIM) * keys,
            bytes_accessed=4 * tok * width + 4 * keys * HEAD_DIM,
        ),
    )(*tables, q, *shared, *state)


def choose_kernel(parent, pieces_ref, o_ref):
    for b in range(o_ref.shape[0]):
        o_ref[b] = pieces_ref[jnp.maximum(parent[b], 0)]


def exchange(a, axes):
    return lax.all_to_all(a, axes, split_axis=0, concat_axis=0, tiled=True)


def shifted(a, axis, step):
    n = lax.axis_size(axis)
    return lax.ppermute(a, axis, [(i, (i + step) % n) for i in range(n)])


def body(queries, branch_keys, branch_values, prompt_keys, prompt_values, parent, fork, lengths):
    tok, width = queries.shape
    heads = width // HEAD_DIM
    rows = prompt_keys.shape[0]
    ny, nh, nb = lax.axis_size("y"), lax.axis_size(HEAD), lax.axis_size(BRANCH)
    unit = 2 * tok // nb
    me = lax.axis_index(BRANCH).reshape(1)

    split = lambda a: a.reshape(rows, nh, HEAD_DIM).transpose(1, 0, 2)
    mine = jnp.concatenate([split(prompt_keys), split(prompt_values)], 1)
    spread = jnp.broadcast_to(mine[None], (ny,) + mine.shape)
    line = exchange(spread.reshape(ny * nh, 2 * rows, HEAD_DIM), ("y",) + HEAD)
    half = ny * nh * rows
    part = lambda a: a.reshape(half, HEAD_DIM)
    line = jnp.concatenate([part(line[:, :rows]), part(line[:, rows:])], 0)
    other = shifted(line, "zl", 1)
    block = jnp.stack([line, other])
    blocks = [block] + [shifted(block, "x", step) for step in range(1, lax.axis_size("x"))]

    own = jnp.concatenate([branch_keys, branch_values], 0)
    pieces = exchange(own.reshape(nb, unit, HEAD_DIM), BRANCH)
    chosen = pl.pallas_call(
        choose_kernel,
        name="choose",
        out_shape=jax.ShapeDtypeStruct((nb, unit, HEAD_DIM), jnp.bfloat16),
        in_specs=[
            pl.BlockSpec(memory_space=pltpu.SMEM),
            pl.BlockSpec(memory_space=pltpu.VMEM),
        ],
        out_specs=pl.BlockSpec(memory_space=pltpu.VMEM),
        compiler_params=pltpu.CompilerParams(vmem_limit_bytes=4 << 20),
    )(parent, pieces)
    above = exchange(chosen, BRANCH).reshape(2 * tok, HEAD_DIM)

    state = (
        jax.ShapeDtypeStruct((tok, width), jnp.float32),
        jax.ShapeDtypeStruct((tok, HEAD_DIM), jnp.float32),
    )
    bound = lambda kernel: functools.partial(kernel, heads=heads)
    keys = len(blocks) * 2 * half
    carried = attention(
        bound(prompt_kernel),
        queries,
        (),
        (*blocks, branch_keys, branch_values),
        (),
        state,
        keys + tok,
        4,
        [pltpu.VMEM((keys, HEAD_DIM), jnp.bfloat16)] * 2,
    )
    out = jax.ShapeDtypeStruct((tok, width), jnp.bfloat16)
    return attention(
        bound(last_kernel), queries, (me, fork, lengths), (above,), carried, out, tok, 8
    )


def solution(mesh):
    fine = Mesh(mesh.devices.reshape(4, 2, 8, 4, 2), BRANCH + HEAD)
    placed = (
        P(BRANCH, HEAD),
        P(BRANCH, HEAD),
        P(BRANCH, HEAD),
        P(BRANCH + HEAD, None),
        P(BRANCH + HEAD, None),
        P(),
        P(),
        P(),
    )

    return jax.shard_map(
        body, mesh=fine, in_specs=placed, out_specs=P(BRANCH, HEAD), check_vma=False
    )
```

```python
import math

import jax
import jax.numpy as jnp
from jax import lax
from jax.experimental import pallas as pl
from jax.experimental.pallas import tpu as pltpu
from jax.sharding import Mesh, PartitionSpec as P


HEAD_DIM = 128
SCALE2 = math.log2(math.e) / math.sqrt(HEAD_DIM)
NEG = -1e30
CHUNK = 512
GROUP = 4
BRANCH = ("x", "zl", "y")
HEAD = ("zh", "c")
CONTRACT_LAST = (((1,), (1,)), ((), ()))
CONTRACT_MID = (((1,), (0,)), ((), ()))


def absorb(q, parts, state):
    for k, v, mask in parts:
        s = lax.dot_general(q, k, CONTRACT_LAST, preferred_element_type=jnp.float32)
        if mask is not None:
            s = jnp.where(mask, s, NEG)
        top = jnp.max(s, axis=1, keepdims=True)
        if state is not None:
            top = jnp.maximum(state[0], top)
        w = jnp.exp2((s - top) * SCALE2).astype(jnp.bfloat16)
        both = lax.dot_general(
            w,
            jnp.concatenate([v, jnp.ones_like(v)], 1),
            CONTRACT_MID,
            preferred_element_type=jnp.float32,
        )
        acc, total = both[:, :HEAD_DIM], both[:, HEAD_DIM:]
        if state is not None:
            fade = jnp.exp2((state[0] - top) * SCALE2)
            total += state[1] * fade
            acc += state[2] * fade
        state = (top, total, acc)
    return state


def lanes(first, count):
    return pl.ds(pl.multiple_of(first * HEAD_DIM, HEAD_DIM), count * HEAD_DIM)


def stacked(ref, step):
    return jnp.concatenate([ref[:, lanes(step * GROUP + i, 1)] for i in range(GROUP)], 0)


def split_rows(a):
    tok = a.shape[0] // GROUP
    return [a[i * tok : (i + 1) * tok] for i in range(GROUP)]


def store_state(state, acc_ref, stat_ref, step):
    top, total, acc = (split_rows(a) for a in state)
    heads = acc_ref.shape[1] // HEAD_DIM
    stat = stat_ref[...]
    lane = lax.broadcasted_iota(jnp.int32, stat.shape, 1)
    for i in range(GROUP):
        head = step * GROUP + i
        acc_ref[:, lanes(head, 1)] = acc[i]
        stat = jnp.where(lane == head, top[i], stat)
        stat = jnp.where(lane == heads + head, total[i], stat)
    stat_ref[...] = stat


def load_state(acc_ref, stat_ref, step):
    heads = acc_ref.shape[1] // HEAD_DIM
    stat = stat_ref[...]
    lane = lax.broadcasted_iota(jnp.int32, stat.shape, 1)
    pick = lambda j: jnp.sum(jnp.where(lane == j, stat, 0.0), axis=1, keepdims=True)
    top = jnp.concatenate([pick(step * GROUP + i) for i in range(GROUP)], 0)
    total = jnp.concatenate([pick(heads + step * GROUP + i) for i in range(GROUP)], 0)
    return top, total, stacked(acc_ref, step)


def gather_rows(blocks, keys, values):
    start = 0
    for block in blocks:
        half = block.shape[1] // 2
        for i in range(block.shape[0]):
            keys[start : start + half] = block[i, :half]
            values[start : start + half] = block[i, half:]
            start += half


def chunks(keys, values):
    ends = range(0, keys.shape[0], CHUNK)
    return [(keys[i : i + CHUNK], values[i : i + CHUNK], None) for i in ends]


def most_kernel(q_ref, *refs):
    blocks, (own_k, own_v, acc_ref, stat_ref, keys, values) = refs[:-6], refs[-6:]
    tok, width = q_ref.shape
    gather_rows(blocks, keys, values)
    stat_ref[...] = jnp.zeros_like(stat_ref)

    @pl.loop(0, width // HEAD_DIM // GROUP)
    def _(step):
        q = stacked(q_ref, step)
        shape = (q.shape[0], tok)
        row = lax.rem(lax.broadcasted_iota(jnp.int32, shape, 0), tok)
        causal = lax.broadcasted_iota(jnp.int32, shape, 1) <= row
        parts = chunks(keys, values) + [(own_k[...], own_v[...], causal)]
        store_state(absorb(q, parts, None), acc_ref, stat_ref, step)


def last_kernel(me, tables, q_ref, far_ref, above_ref, acc_in, stat_in, o_ref, keys, values):
    tok, width = q_ref.shape
    count = tables.shape[0] // 3
    fork, live = tables[count + me[0]], tables[2 * count + me[0]]
    gather_rows([far_ref], keys, values)

    @pl.loop(0, width // HEAD_DIM // GROUP)
    def _(step):
        q = stacked(q_ref, step)
        seen = lax.broadcasted_iota(jnp.int32, (q.shape[0], tok), 1) < fork
        parts = chunks(keys, values) + [(above_ref[:tok], above_ref[tok:], seen)]
        _, total, acc = absorb(q, parts, load_state(acc_in, stat_in, step))
        kept = lax.broadcasted_iota(jnp.int32, (tok, HEAD_DIM), 0) < live
        for i, out in enumerate(split_rows(acc / total)):
            at = lanes(step * GROUP + i, 1)
            o_ref[:, at] = jnp.where(kept, out, 0.0).astype(o_ref.dtype)


def attention(kernel, tables, arrays, outs, keys, scratch_rows):
    tok, width = arrays[0].shape
    vmem = pl.BlockSpec(memory_space=pltpu.VMEM)
    smem = pl.BlockSpec(memory_space=pltpu.SMEM)
    return pl.pallas_call(
        kernel,
        out_shape=outs,
        in_specs=[smem] * len(tables) + [vmem] * len(arrays),
        out_specs=jax.tree.map(lambda _: vmem, outs),
        scratch_shapes=[pltpu.VMEM((scratch_rows, HEAD_DIM), jnp.bfloat16)] * 2,
        compiler_params=pltpu.CompilerParams(vmem_limit_bytes=32 << 20),
        cost_estimate=pl.CostEstimate(
            flops=4 * tok * width * keys,
            transcendentals=tok * (width // HEAD_DIM) * keys,
            bytes_accessed=4 * tok * width + 4 * keys * HEAD_DIM,
        ),
    )(*tables, *arrays)


def choose_kernel(parent, pieces_ref, o_ref):
    for b in range(o_ref.shape[0]):
        o_ref[b] = pieces_ref[jnp.maximum(parent[b], 0)]


def exchange(a, axes):
    return lax.all_to_all(a, axes, split_axis=0, concat_axis=0, tiled=True)


def shifted(a, axis, step):
    n = lax.axis_size(axis)
    return lax.ppermute(a, axis, [(i, (i + step) % n) for i in range(n)])


def body(queries, branch_keys, branch_values, prompt_keys, prompt_values, parent, fork, lengths):
    tok, width = queries.shape
    rows = prompt_keys.shape[0]
    ny, nz, nc, nb = (lax.axis_size(a) for a in ("y", "zh", "c", BRANCH))
    unit = 2 * tok // nb
    me = lax.axis_index(BRANCH).reshape(1)
    first_core = lax.axis_index("c") == 0
    tables = jnp.concatenate([parent, fork, lengths])

    both = jnp.stack([prompt_keys, prompt_values]).reshape(2, rows, nz, nc, HEAD_DIM)
    kept = jnp.where(first_core, both[:, :, :, 0], both[:, :, :, 1])
    given = jnp.where(first_core, both[:, :, :, 1], both[:, :, :, 0])
    taken = shifted(given, "c", 1)
    mine = jnp.concatenate([kept, taken], 1).transpose(2, 0, 1, 3)
    mine = mine.reshape(nz, 2 * nc * rows, HEAD_DIM)
    spread = jnp.broadcast_to(mine[None], (ny,) + mine.shape)
    line = exchange(spread.reshape(ny * nz, 2 * nc * rows, HEAD_DIM), ("y", "zh"))
    half = ny * nz * nc * rows
    part = lambda a: a.reshape(half, HEAD_DIM)
    line = jnp.concatenate([part(line[:, : nc * rows]), part(line[:, nc * rows :])], 0)
    other = shifted(line, "zl", 1)
    block = jnp.stack([line, other])
    near = [block, shifted(block, "x", 1), shifted(block, "x", -1)]
    far = shifted(block, "x", 2)

    own = jnp.concatenate([branch_keys, branch_values], 0).reshape(nb, unit, HEAD_DIM)
    pieces = exchange(own, BRANCH)
    chosen = pl.pallas_call(
        choose_kernel,
        name="choose",
        out_shape=jax.ShapeDtypeStruct((nb, unit, HEAD_DIM), jnp.bfloat16),
        in_specs=[
            pl.BlockSpec(memory_space=pltpu.SMEM),
            pl.BlockSpec(memory_space=pltpu.VMEM),
        ],
        out_specs=pl.BlockSpec(memory_space=pltpu.VMEM),
        compiler_params=pltpu.CompilerParams(vmem_limit_bytes=4 << 20),
    )(tables, pieces)
    above = exchange(chosen, BRANCH).reshape(2 * tok, HEAD_DIM)

    state = (
        jax.ShapeDtypeStruct((tok, width), jnp.float32),
        jax.ShapeDtypeStruct((tok, HEAD_DIM), jnp.float32),
    )
    keys = len(near) * 2 * half
    carried = attention(
        most_kernel, (), (queries, *near, branch_keys, branch_values), state, keys + tok, keys
    )
    out = jax.ShapeDtypeStruct((tok, width), jnp.bfloat16)
    arrays = (queries, far, above, *carried)
    return attention(last_kernel, (me, tables), arrays, out, 2 * half + tok, 2 * half)


def solution(mesh):
    fine = Mesh(mesh.devices.reshape(4, 2, 8, 4, 2), BRANCH + HEAD)
    placed = (
        P(BRANCH, HEAD),
        P(BRANCH, HEAD),
        P(BRANCH, HEAD),
        P(BRANCH + HEAD, None),
        P(BRANCH + HEAD, None),
        P(),
        P(),
        P(),
    )

    return jax.shard_map(
        body, mesh=fine, in_specs=placed, out_specs=P(BRANCH, HEAD), check_vma=False
    )
```

```python
import functools
import math

import jax
import jax.numpy as jnp
from jax import lax
from jax.experimental import pallas as pl
from jax.experimental.pallas import tpu as pltpu
from jax.sharding import Mesh, PartitionSpec as P


HEAD_DIM = 128
SCALE2 = math.log2(math.e) / math.sqrt(HEAD_DIM)
NEG = -1e30
CHUNK = 512
BRANCH = ("x", "zl", "y")
HEAD = ("zh", "c")
CONTRACT_LAST = (((1,), (1,)), ((), ()))
CONTRACT_MID = (((1,), (0,)), ((), ()))


def absorb(q, parts, state):
    for k, v, mask in parts:
        s = lax.dot_general(q, k, CONTRACT_LAST, preferred_element_type=jnp.float32)
        if mask is not None:
            s = jnp.where(mask, s, NEG)
        top = jnp.max(s, axis=1, keepdims=True)
        if state is not None:
            top = jnp.maximum(state[0], top)
        w = jnp.exp2((s - top) * SCALE2).astype(jnp.bfloat16)
        both = lax.dot_general(
            w,
            jnp.concatenate([v, jnp.ones_like(v)], 1),
            CONTRACT_MID,
            preferred_element_type=jnp.float32,
        )
        acc, total = both[:, :HEAD_DIM], both[:, HEAD_DIM:]
        if state is not None:
            fade = jnp.exp2((state[0] - top) * SCALE2)
            total += state[1] * fade
            acc += state[2] * fade
        state = (top, total, acc)
    return state


def stacked(ref):
    return jnp.concatenate(
        [ref[:, i : i + HEAD_DIM] for i in range(0, ref.shape[1], HEAD_DIM)], 0
    )


def store_state(state, acc_ref, stat_ref, heads):
    top, total, acc = state
    tok = acc_ref.shape[0]
    here = acc_ref.shape[1] // HEAD_DIM
    step = pl.program_id(0)
    lane = lax.broadcasted_iota(jnp.int32, (tok, HEAD_DIM), 1)
    stat = stat_ref[...]
    for i in range(here):
        at = slice(i * tok, (i + 1) * tok)
        acc_ref[:, i * HEAD_DIM : (i + 1) * HEAD_DIM] = acc[at]
        stat = jnp.where(lane == step * here + i, top[at], stat)
        stat = jnp.where(lane == heads + step * here + i, total[at], stat)
    stat_ref[...] = stat


def load_state(acc_ref, stat_ref, heads):
    here = acc_ref.shape[1] // HEAD_DIM
    step = pl.program_id(0)
    stat = stat_ref[...]
    lane = lax.broadcasted_iota(jnp.int32, stat.shape, 1)
    pick = lambda j: jnp.sum(jnp.where(lane == j, stat, 0.0), axis=1, keepdims=True)
    top = jnp.concatenate([pick(step * here + i) for i in range(here)], 0)
    total = jnp.concatenate([pick(heads + step * here + i) for i in range(here)], 0)
    return top, total, stacked(acc_ref)


def prompt_kernel(q_ref, *refs, heads):
    blocks, (own_k, own_v, acc_ref, stat_ref, keys, values) = refs[:-6], refs[-6:]
    tok = q_ref.shape[0]

    @pl.when(pl.program_id(0) == 0)
    def _():
        start = 0
        for block in blocks:
            half = block.shape[1] // 2
            for i in range(block.shape[0]):
                keys[start : start + half] = block[i, :half]
                values[start : start + half] = block[i, half:]
                start += half

    q = stacked(q_ref)
    shape = (q.shape[0], tok)
    row = lax.rem(lax.broadcasted_iota(jnp.int32, shape, 0), tok)
    causal = lax.broadcasted_iota(jnp.int32, shape, 1) <= row
    parts = [
        (keys[i : i + CHUNK], values[i : i + CHUNK], None) for i in range(0, keys.shape[0], CHUNK)
    ]
    parts.append((own_k[...], own_v[...], causal))
    store_state(absorb(q, parts, None), acc_ref, stat_ref, heads)


def last_kernel(me, tables, q_ref, above_ref, acc_in, stat_in, o_ref, *, heads):
    tok = q_ref.shape[0]
    count = tables.shape[0] // 3
    fork, live = tables[count + me[0]], tables[2 * count + me[0]]
    q = stacked(q_ref)
    seen = lax.broadcasted_iota(jnp.int32, (q.shape[0], tok), 1) < fork
    parts = [(above_ref[:tok], above_ref[tok:], seen)]
    _, total, acc = absorb(q, parts, load_state(acc_in, stat_in, heads))
    kept = lax.broadcasted_iota(jnp.int32, (tok, HEAD_DIM), 0) < live
    out = acc / total
    for i in range(q_ref.shape[1] // HEAD_DIM):
        at = slice(i * HEAD_DIM, (i + 1) * HEAD_DIM)
        o_ref[:, at] = jnp.where(kept, out[i * tok : (i + 1) * tok], 0.0).astype(o_ref.dtype)


def attention(kernel, q, tables, shared, state, outs, keys, per_step, scratch=()):
    tok, width = q.shape
    step = per_step * HEAD_DIM
    fixed = lambda a: pl.BlockSpec(a.shape, lambda h, *_: (0,) * a.ndim)
    moving = pl.BlockSpec((tok, step), lambda h, *_: (0, h))
    spec = lambda a: moving if a.shape[1] == width else fixed(a)
    return pl.pallas_call(
        kernel,
        out_shape=outs,
        grid_spec=pltpu.PrefetchScalarGridSpec(
            num_scalar_prefetch=len(tables),
            grid=(width // step,),
            in_specs=[moving] + [fixed(a) for a in shared] + [spec(a) for a in state],
            out_specs=jax.tree.map(spec, outs),
            scratch_shapes=scratch,
        ),
        compiler_params=pltpu.CompilerParams(vmem_limit_bytes=40 << 20),
        cost_estimate=pl.CostEstimate(
            flops=4 * tok * width * keys,
            transcendentals=tok * (width // HEAD_DIM) * keys,
            bytes_accessed=4 * tok * width + 4 * keys * HEAD_DIM,
        ),
    )(*tables, q, *shared, *state)


def choose_kernel(parent, pieces_ref, o_ref):
    for b in range(o_ref.shape[0]):
        o_ref[b] = pieces_ref[jnp.maximum(parent[b], 0)]


def exchange(a, axes):
    return lax.all_to_all(a, axes, split_axis=0, concat_axis=0, tiled=True)


def shifted(a, axis, step):
    n = lax.axis_size(axis)
    return lax.ppermute(a, axis, [(i, (i + step) % n) for i in range(n)])


def body(queries, branch_keys, branch_values, prompt_keys, prompt_values, parent, fork, lengths):
    tok, width = queries.shape
    heads = width // HEAD_DIM
    rows = prompt_keys.shape[0]
    ny, nh, nb = lax.axis_size("y"), lax.axis_size(HEAD), lax.axis_size(BRANCH)
    unit = 2 * tok // nb
    me = lax.axis_index(BRANCH).reshape(1)
    tables = jnp.concatenate([parent, fork, lengths])

    split = lambda a: a.reshape(rows, nh, HEAD_DIM).transpose(1, 0, 2)
    mine = jnp.concatenate([split(prompt_keys), split(prompt_values)], 1)
    spread = jnp.broadcast_to(mine[None], (ny,) + mine.shape)
    line = exchange(spread.reshape(ny * nh, 2 * rows, HEAD_DIM), ("y",) + HEAD)
    half = ny * nh * rows
    part = lambda a: a.reshape(half, HEAD_DIM)
    line = jnp.concatenate([part(line[:, :rows]), part(line[:, rows:])], 0)
    other = shifted(line, "zl", 1)
    block = jnp.stack([line, other])
    blocks = [block] + [shifted(block, "x", step) for step in range(1, lax.axis_size("x"))]

    own = jnp.concatenate([branch_keys, branch_values], 0).reshape(nb, unit, HEAD_DIM)
    pieces = exchange(own, BRANCH)
    chosen = pl.pallas_call(
        choose_kernel,
        name="choose",
        out_shape=jax.ShapeDtypeStruct((nb, unit, HEAD_DIM), jnp.bfloat16),
        in_specs=[
            pl.BlockSpec(memory_space=pltpu.SMEM),
            pl.BlockSpec(memory_space=pltpu.VMEM),
        ],
        out_specs=pl.BlockSpec(memory_space=pltpu.VMEM),
        compiler_params=pltpu.CompilerParams(vmem_limit_bytes=4 << 20),
    )(tables, pieces)
    above = exchange(chosen, BRANCH).reshape(2 * tok, HEAD_DIM)

    state = (
        jax.ShapeDtypeStruct((tok, width), jnp.float32),
        jax.ShapeDtypeStruct((tok, HEAD_DIM), jnp.float32),
    )
    bound = lambda kernel: functools.partial(kernel, heads=heads)
    keys = len(blocks) * 2 * half
    carried = attention(
        bound(prompt_kernel),
        queries,
        (),
        (*blocks, branch_keys, branch_values),
        (),
        state,
        keys + tok,
        4,
        [pltpu.VMEM((keys, HEAD_DIM), jnp.bfloat16)] * 2,
    )
    out = jax.ShapeDtypeStruct((tok, width), jnp.bfloat16)
    return attention(bound(last_kernel), queries, (me, tables), (above,), carried, out, tok, 8)


def solution(mesh):
    fine = Mesh(mesh.devices.reshape(4, 2, 8, 4, 2), BRANCH + HEAD)
    placed = (
        P(BRANCH, HEAD),
        P(BRANCH, HEAD),
        P(BRANCH, HEAD),
        P(BRANCH + HEAD, None),
        P(BRANCH + HEAD, None),
        P(),
        P(),
        P(),
    )

    return jax.shard_map(
        body, mesh=fine, in_specs=placed, out_specs=P(BRANCH, HEAD), check_vma=False
    )
```

```python
import math

import jax
import jax.numpy as jnp
from jax import lax
from jax.experimental import pallas as pl
from jax.experimental.pallas import tpu as pltpu
from jax.sharding import Mesh, PartitionSpec as P


HEAD_DIM = 128
SCALE2 = math.log2(math.e) / math.sqrt(HEAD_DIM)
NEG = -1e30
CHUNK = 512
GROUP = 4
BRANCH = ("x", "zl", "y")
HEAD = ("zh", "c")
CONTRACT_LAST = (((1,), (1,)), ((), ()))
CONTRACT_MID = (((1,), (0,)), ((), ()))


def absorb(q, parts, state):
    for k, v, mask in parts:
        s = lax.dot_general(q, k, CONTRACT_LAST, preferred_element_type=jnp.float32)
        if mask is not None:
            s = jnp.where(mask, s, NEG)
        top = jnp.max(s, axis=1, keepdims=True)
        if state is not None:
            top = jnp.maximum(state[0], top)
        w = jnp.exp2((s - top) * SCALE2).astype(jnp.bfloat16)
        both = lax.dot_general(
            w,
            jnp.concatenate([v, jnp.ones_like(v)], 1),
            CONTRACT_MID,
            preferred_element_type=jnp.float32,
        )
        acc, total = both[:, :HEAD_DIM], both[:, HEAD_DIM:]
        if state is not None:
            fade = jnp.exp2((state[0] - top) * SCALE2)
            total += state[1] * fade
            acc += state[2] * fade
        state = (top, total, acc)
    return state


def lanes(first, count):
    return slice(first * HEAD_DIM, (first + count) * HEAD_DIM)


def stacked(ref, step):
    return jnp.concatenate([ref[:, lanes(step * GROUP + i, 1)] for i in range(GROUP)], 0)


def split_rows(a):
    tok = a.shape[0] // GROUP
    return [a[i * tok : (i + 1) * tok] for i in range(GROUP)]


def store_state(state, out_ref, level_ref, step):
    top, total, acc = state
    levels = level_ref[...]
    lane = lax.broadcasted_iota(jnp.int32, levels.shape, 1)
    outs, own = split_rows(acc / total), split_rows(top * SCALE2 + jnp.log2(total))
    for i in range(GROUP):
        out_ref[:, lanes(step * GROUP + i, 1)] = outs[i]
        levels = jnp.where(lane == step * GROUP + i, own[i], levels)
    level_ref[...] = levels


def gather_rows(blocks, keys, values):
    start = 0
    for block in blocks:
        half = block.shape[1] // 2
        for i in range(block.shape[0]):
            keys[start : start + half] = block[i, :half]
            values[start : start + half] = block[i, half:]
            start += half


def chunks(keys, values):
    ends = range(0, keys.shape[0], CHUNK)
    return [(keys[i : i + CHUNK], values[i : i + CHUNK], None) for i in ends]


def most_kernel(q_ref, *refs):
    blocks, (own_k, own_v, out_ref, level_ref, keys, values) = refs[:-6], refs[-6:]
    tok, width = q_ref.shape
    gather_rows(blocks, keys, values)
    level_ref[...] = jnp.zeros_like(level_ref)

    for step in range(width // HEAD_DIM // GROUP):
        q = stacked(q_ref, step)
        shape = (q.shape[0], tok)
        row = lax.rem(lax.broadcasted_iota(jnp.int32, shape, 0), tok)
        causal = lax.broadcasted_iota(jnp.int32, shape, 1) <= row
        parts = chunks(keys, values) + [(own_k[...], own_v[...], causal)]
        store_state(absorb(q, parts, None), out_ref, level_ref, step)


def last_kernel(me, tables, q_ref, above_ref, *refs):
    far, (out_in, level_in, o_ref, keys, values) = refs[:-5], refs[-5:]
    tok, width = q_ref.shape
    count = tables.shape[0] // 3
    fork, live = tables[count + me[0]], tables[2 * count + me[0]]
    gather_rows(far, keys, values)
    kept = lax.broadcasted_iota(jnp.int32, (tok, HEAD_DIM), 0) < live

    for step in range(width // HEAD_DIM // GROUP):
        q = stacked(q_ref, step)
        seen = lax.broadcasted_iota(jnp.int32, (q.shape[0], tok), 1) < fork
        parts = chunks(keys, values) if far else []
        parts.append((above_ref[:tok], above_ref[tok:], seen))
        peak, extra, more = absorb(q, parts, None)
        peak = jnp.broadcast_to(peak * SCALE2, more.shape)
        levels = level_in[...]
        pick = lambda j: jnp.broadcast_to(levels[:, j : j + 1], (tok, HEAD_DIM))
        level = jnp.concatenate([pick(step * GROUP + i) for i in range(GROUP)], 0)
        top = jnp.maximum(level, peak)
        old, new = jnp.exp2(level - top), jnp.exp2(peak - top)
        out = (stacked(out_in, step) * old + more * new) / (old + extra * new)
        for i, part in enumerate(split_rows(out)):
            at = lanes(step * GROUP + i, 1)
            o_ref[:, at] = jnp.where(kept, part, 0.0).astype(o_ref.dtype)


def attention(kernel, tables, arrays, outs, keys, scratch_rows):
    tok, width = arrays[0].shape
    vmem = pl.BlockSpec(memory_space=pltpu.VMEM)
    smem = pl.BlockSpec(memory_space=pltpu.SMEM)
    return pl.pallas_call(
        kernel,
        out_shape=outs,
        in_specs=[smem] * len(tables) + [vmem] * len(arrays),
        out_specs=jax.tree.map(lambda _: vmem, outs),
        scratch_shapes=[pltpu.VMEM((scratch_rows, HEAD_DIM), jnp.bfloat16)] * 2,
        compiler_params=pltpu.CompilerParams(vmem_limit_bytes=32 << 20),
        cost_estimate=pl.CostEstimate(
            flops=4 * tok * width * keys,
            transcendentals=tok * (width // HEAD_DIM) * keys,
            bytes_accessed=4 * tok * width + 4 * keys * HEAD_DIM,
        ),
    )(*tables, *arrays)


def choose_kernel(parent, pieces_ref, o_ref):
    for b in range(o_ref.shape[0]):
        o_ref[b] = pieces_ref[jnp.maximum(parent[b], 0)]


def exchange(a, axes):
    return lax.all_to_all(a, axes, split_axis=0, concat_axis=0, tiled=True)


def shifted(a, axis, step):
    n = lax.axis_size(axis)
    return lax.ppermute(a, axis, [(i, (i + step) % n) for i in range(n)])


def body(queries, branch_keys, branch_values, prompt_keys, prompt_values, parent, fork, lengths):
    tok, width = queries.shape
    rows = prompt_keys.shape[0]
    ny, nh, nb = lax.axis_size("y"), lax.axis_size(HEAD), lax.axis_size(BRANCH)
    unit = 2 * tok // nb
    me = lax.axis_index(BRANCH).reshape(1)
    tables = jnp.concatenate([parent, fork, lengths])

    split = lambda a: a.reshape(rows, nh, HEAD_DIM).transpose(1, 0, 2)
    mine = jnp.concatenate([split(prompt_keys), split(prompt_values)], 1)
    spread = jnp.broadcast_to(mine[None], (ny,) + mine.shape)
    line = exchange(spread.reshape(ny * nh, 2 * rows, HEAD_DIM), ("y",) + HEAD)
    half = ny * nh * rows
    part = lambda a: a.reshape(half, HEAD_DIM)
    line = jnp.concatenate([part(line[:, :rows]), part(line[:, rows:])], 0)
    other = shifted(line, "zl", 1)
    block = jnp.stack([line, other])
    near = [block, shifted(block, "x", 1), shifted(block, "x", -1)]
    far = shifted(block, "x", 2)

    own = jnp.concatenate([branch_keys, branch_values], 0).reshape(nb, unit, HEAD_DIM)
    pieces = exchange(own, BRANCH)
    chosen = pl.pallas_call(
        choose_kernel,
        name="choose",
        out_shape=jax.ShapeDtypeStruct((nb, unit, HEAD_DIM), jnp.bfloat16),
        in_specs=[
            pl.BlockSpec(memory_space=pltpu.SMEM),
            pl.BlockSpec(memory_space=pltpu.VMEM),
        ],
        out_specs=pl.BlockSpec(memory_space=pltpu.VMEM),
        compiler_params=pltpu.CompilerParams(vmem_limit_bytes=4 << 20),
    )(tables, pieces)
    above = exchange(chosen, BRANCH).reshape(2 * tok, HEAD_DIM)

    wide = jax.ShapeDtypeStruct((tok, width), jnp.float32)
    level = jax.ShapeDtypeStruct((tok, HEAD_DIM), jnp.float32)
    keys = len(near) * 2 * half
    state = attention(
        most_kernel,
        (),
        (queries, *near, branch_keys, branch_values),
        (wide, level),
        keys + tok,
        keys,
    )
    out = jax.ShapeDtypeStruct((tok, width), jnp.bfloat16)
    arrays = (queries, above, far, *state)
    return attention(last_kernel, (me, tables), arrays, out, 2 * half + tok, 2 * half)


def solution(mesh):
    fine = Mesh(mesh.devices.reshape(4, 2, 8, 4, 2), BRANCH + HEAD)
    placed = (
        P(BRANCH, HEAD),
        P(BRANCH, HEAD),
        P(BRANCH, HEAD),
        P(BRANCH + HEAD, None),
        P(BRANCH + HEAD, None),
        P(),
        P(),
        P(),
    )

    return jax.shard_map(
        body, mesh=fine, in_specs=placed, out_specs=P(BRANCH, HEAD), check_vma=False
    )
```

```python
import math

import jax
import jax.numpy as jnp
from jax import lax
from jax.experimental import pallas as pl
from jax.experimental.pallas import tpu as pltpu
from jax.sharding import Mesh, PartitionSpec as P


HEAD_DIM = 128
SCALE2 = math.log2(math.e) / math.sqrt(HEAD_DIM)
NEG = -1e30
CHUNK = 512
GROUP = 4
BRANCH = ("x", "zl", "y")
HEAD = ("zh", "c")
CONTRACT_LAST = (((1,), (1,)), ((), ()))
CONTRACT_MID = (((1,), (0,)), ((), ()))


def absorb(q, parts, state):
    for k, v, mask in parts:
        s = lax.dot_general(q, k, CONTRACT_LAST, preferred_element_type=jnp.float32)
        if mask is not None:
            s = jnp.where(mask, s, NEG)
        top = jnp.max(s, axis=1, keepdims=True)
        if state is not None:
            top = jnp.maximum(state[0], top)
        w = jnp.exp2((s - top) * SCALE2).astype(jnp.bfloat16)
        both = lax.dot_general(
            w,
            jnp.concatenate([v, jnp.ones_like(v)], 1),
            CONTRACT_MID,
            preferred_element_type=jnp.float32,
        )
        acc, total = both[:, :HEAD_DIM], both[:, HEAD_DIM:]
        if state is not None:
            fade = jnp.exp2((state[0] - top) * SCALE2)
            total += state[1] * fade
            acc += state[2] * fade
        state = (top, total, acc)
    return state


def lanes(first, count):
    return slice(first * HEAD_DIM, (first + count) * HEAD_DIM)


def stacked(ref, step):
    return jnp.concatenate([ref[:, lanes(step * GROUP + i, 1)] for i in range(GROUP)], 0)


def split_rows(a):
    tok = a.shape[0] // GROUP
    return [a[i * tok : (i + 1) * tok] for i in range(GROUP)]


def merged(state, mean_in, level_in, step):
    peak, extra, more = state
    peak = jnp.broadcast_to(peak * SCALE2, more.shape)
    if mean_in is None:
        return more / extra, peak + jnp.log2(extra)
    tok = level_in.shape[0]
    levels = level_in[...]
    pick = lambda j: jnp.broadcast_to(levels[:, j : j + 1], (tok, HEAD_DIM))
    level = jnp.concatenate([pick(step * GROUP + i) for i in range(GROUP)], 0)
    top = jnp.maximum(level, peak)
    old, new = jnp.exp2(level - top), jnp.exp2(peak - top)
    total = old + extra * new
    return (stacked(mean_in, step) * old + more * new) / total, top + jnp.log2(total)


def store_state(mean, level, mean_ref, level_ref, step):
    levels = level_ref[...]
    lane = lax.broadcasted_iota(jnp.int32, levels.shape, 1)
    means, own = split_rows(mean), split_rows(level)
    for i in range(GROUP):
        mean_ref[:, lanes(step * GROUP + i, 1)] = means[i].astype(mean_ref.dtype)
        levels = jnp.where(lane == step * GROUP + i, own[i], levels)
    level_ref[...] = levels


def gather_rows(blocks, keys, values):
    start = 0
    for block in blocks:
        half = block.shape[1] // 2
        for i in range(block.shape[0]):
            keys[start : start + half] = block[i, :half]
            values[start : start + half] = block[i, half:]
            start += half


def chunks(keys, values):
    ends = range(0, keys.shape[0], CHUNK)
    return [(keys[i : i + CHUNK], values[i : i + CHUNK], None) for i in ends]


def own_kernel(q_ref, block, own_k, own_v, mean_ref, level_ref, keys, values):
    tok, width = q_ref.shape
    gather_rows([block], keys, values)
    level_ref[...] = jnp.zeros_like(level_ref)
    for step in range(width // HEAD_DIM // GROUP):
        q = stacked(q_ref, step)
        shape = (q.shape[0], tok)
        row = lax.rem(lax.broadcasted_iota(jnp.int32, shape, 0), tok)
        causal = lax.broadcasted_iota(jnp.int32, shape, 1) <= row
        parts = chunks(keys, values) + [(own_k[...], own_v[...], causal)]
        mean, level = merged(absorb(q, parts, None), None, None, step)
        store_state(mean, level, mean_ref, level_ref, step)


def most_kernel(q_ref, left, right, mean_in, level_in, mean_ref, level_ref, keys, values):
    _, width = q_ref.shape
    gather_rows([left, right], keys, values)
    level_ref[...] = jnp.zeros_like(level_ref)
    for step in range(width // HEAD_DIM // GROUP):
        state = absorb(stacked(q_ref, step), chunks(keys, values), None)
        mean, level = merged(state, mean_in, level_in, step)
        store_state(mean, level, mean_ref, level_ref, step)


def last_kernel(me, tables, q_ref, above_ref, far, mean_in, level_in, o_ref, keys, values):
    tok, width = q_ref.shape
    count = tables.shape[0] // 3
    fork, live = tables[count + me[0]], tables[2 * count + me[0]]
    gather_rows([far], keys, values)
    kept = lax.broadcasted_iota(jnp.int32, (tok, HEAD_DIM), 0) < live
    for step in range(width // HEAD_DIM // GROUP):
        q = stacked(q_ref, step)
        seen = lax.broadcasted_iota(jnp.int32, (q.shape[0], tok), 1) < fork
        parts = chunks(keys, values) + [(above_ref[:tok], above_ref[tok:], seen)]
        out, _ = merged(absorb(q, parts, None), mean_in, level_in, step)
        for i, part in enumerate(split_rows(out)):
            at = lanes(step * GROUP + i, 1)
            o_ref[:, at] = jnp.where(kept, part, 0.0).astype(o_ref.dtype)


def attention(kernel, tables, arrays, outs, keys, scratch_rows):
    tok, width = arrays[0].shape
    vmem = pl.BlockSpec(memory_space=pltpu.VMEM)
    smem = pl.BlockSpec(memory_space=pltpu.SMEM)
    return pl.pallas_call(
        kernel,
        out_shape=outs,
        in_specs=[smem] * len(tables) + [vmem] * len(arrays),
        out_specs=jax.tree.map(lambda _: vmem, outs),
        scratch_shapes=[pltpu.VMEM((scratch_rows, HEAD_DIM), jnp.bfloat16)] * 2,
        compiler_params=pltpu.CompilerParams(vmem_limit_bytes=32 << 20),
        cost_estimate=pl.CostEstimate(
            flops=4 * tok * width * keys,
            transcendentals=tok * (width // HEAD_DIM) * keys,
            bytes_accessed=4 * tok * width + 4 * keys * HEAD_DIM,
        ),
    )(*tables, *arrays)


def choose_kernel(parent, pieces_ref, o_ref):
    for b in range(o_ref.shape[0]):
        o_ref[b] = pieces_ref[jnp.maximum(parent[b], 0)]


def exchange(a, axes):
    return lax.all_to_all(a, axes, split_axis=0, concat_axis=0, tiled=True)


def shifted(a, axis, step):
    n = lax.axis_size(axis)
    return lax.ppermute(a, axis, [(i, (i + step) % n) for i in range(n)])


def body(queries, branch_keys, branch_values, prompt_keys, prompt_values, parent, fork, lengths):
    tok, width = queries.shape
    rows = prompt_keys.shape[0]
    ny, nh, nb = lax.axis_size("y"), lax.axis_size(HEAD), lax.axis_size(BRANCH)
    unit = 2 * tok // nb
    me = lax.axis_index(BRANCH).reshape(1)
    tables = jnp.concatenate([parent, fork, lengths])

    split = lambda a: a.reshape(rows, nh, HEAD_DIM).transpose(1, 0, 2)
    mine = jnp.concatenate([split(prompt_keys), split(prompt_values)], 1)
    spread = jnp.broadcast_to(mine[None], (ny,) + mine.shape)
    line = exchange(spread.reshape(ny * nh, 2 * rows, HEAD_DIM), ("y",) + HEAD)
    half = ny * nh * rows
    part = lambda a: a.reshape(half, HEAD_DIM)
    line = jnp.concatenate([part(line[:, :rows]), part(line[:, rows:])], 0)
    other = shifted(line, "zl", 1)
    block = jnp.stack([line, other])
    near = [shifted(block, "x", 1), shifted(block, "x", -1)]
    far = shifted(block, "x", 2)

    own = jnp.concatenate([branch_keys, branch_values], 0).reshape(nb, unit, HEAD_DIM)
    pieces = exchange(own, BRANCH)
    chosen = pl.pallas_call(
        choose_kernel,
        name="choose",
        out_shape=jax.ShapeDtypeStruct((nb, unit, HEAD_DIM), jnp.bfloat16),
        in_specs=[
            pl.BlockSpec(memory_space=pltpu.SMEM),
            pl.BlockSpec(memory_space=pltpu.VMEM),
        ],
        out_specs=pl.BlockSpec(memory_space=pltpu.VMEM),
        compiler_params=pltpu.CompilerParams(vmem_limit_bytes=4 << 20),
    )(tables, pieces)
    above = exchange(chosen, BRANCH).reshape(2 * tok, HEAD_DIM)

    wide = jax.ShapeDtypeStruct((tok, width), jnp.float32)
    level = jax.ShapeDtypeStruct((tok, HEAD_DIM), jnp.float32)
    narrow = jax.ShapeDtypeStruct((tok, width), jnp.bfloat16)
    keys = 2 * half
    arrays = (queries, block, branch_keys, branch_values)
    state = attention(own_kernel, (), arrays, (narrow, level), keys + tok, keys)
    arrays = (queries, *near, *state)
    state = attention(most_kernel, (), arrays, (wide, level), 2 * keys, 2 * keys)
    out = jax.ShapeDtypeStruct((tok, width), jnp.bfloat16)
    arrays = (queries, above, far, *state)
    return attention(last_kernel, (me, tables), arrays, out, keys + tok, keys)


def solution(mesh):
    fine = Mesh(mesh.devices.reshape(4, 2, 8, 4, 2), BRANCH + HEAD)
    placed = (
        P(BRANCH, HEAD),
        P(BRANCH, HEAD),
        P(BRANCH, HEAD),
        P(BRANCH + HEAD, None),
        P(BRANCH + HEAD, None),
        P(),
        P(),
        P(),
    )

    return jax.shard_map(
        body, mesh=fine, in_specs=placed, out_specs=P(BRANCH, HEAD), check_vma=False
    )
```
